256 devices in a mesh: engine: 16 (over x, z_lo, core), expert: 16 (over z_hi, y).
Axes of the slice: x: 4, y: 4, z: 8 (z_hi: 4, z_lo: 2; z = z_hi * 2 + z_lo), core: 2. Of those that a mesh axis runs over, the one named last changes fastest.
Arguments:
- tokens: bfloat16 [2, 32768, 4096], P(None, ('engine', 'expert')), may hold values from -6 to 6
- expert_ids: int32 [2, 32768, 2], P(None, ('engine', 'expert')), may hold values from 0 to 15, all different within a row; in each aligned block of 128 rows (0 to 127, 128 to 255, ..., all dimensions but the last counted through in order) at most 24 rows name the same one
- route_gain: float32 [2, 32768, 2], P(None, ('engine', 'expert')), may hold values from 0.1 to 1
- gate_up_master: float32 [16, 4096, 1536], P('expert', 'engine'), may hold values from -0.09375 to 0.09375
- gate_up_moment: float32 [16, 4096, 1536], P('expert', 'engine'), may hold values from -0.09375 to 0.09375
- gate_up_grad: bfloat16 [16, 4096, 1536], P('expert', 'engine'), may hold values from -0.09375 to 0.09375
- down_master: float32 [16, 768, 4096], P('expert', None, 'engine'), may hold values from -0.21875 to 0.21875
- down_moment: float32 [16, 768, 4096], P('expert', None, 'engine'), may hold values from -0.21875 to 0.21875
- down_grad: bfloat16 [16, 768, 4096], P('expert', None, 'engine'), may hold values from -0.21875 to 0.21875
Outputs:
- mixed: bfloat16 [2, 32768, 4096], P(None, ('engine', 'expert'))
The draws below stay inside these ranges and needn't reach their ends.
Inputs may be any that keep to these rules, and one draw needn't show every extreme that they name: `expert_ids`: in each aligned block of 128 rows of one step, no expert is named by more than 24 rows, a bound that some block reaches; a row names 2 different experts.
All inputs are finite; a program needn't handle non-finite values.
Results may differ from the reference program's by a relative error of at most 0.0081.
Values may be sent and summed in bfloat16 or wider, within the bound.
No kernel may reach another device: no remote copies, remote signals or barrier semaphores. Data moves between devices by JAX's collectives and lax.ppermute only.
A program may use at most 128 MiB of HBM per device.

```python
import math
import jax
import jax.numpy as jnp
import numpy as np
from jax import lax

D = 4096
FF = 768
TOP = 2
STEPS = 2
ROW_DEV = 128
EXPERTS = 16
CAP = 24
ROWS = 32768
N_ENGINE = 16
N_EXPERT = 16


def level_of(key, dims, shards, least, largest):
    factor_of, own = 1.0, jax.random.fold_in(key, 6)
    for dim, parts in shards:
        heights = jnp.exp(jax.random.uniform(jax.random.fold_in(own, dim), (parts,), jnp.float32, least / len(shards), largest / len(shards)))
        factor_of = factor_of * jnp.repeat(heights, dims[dim] // parts).reshape([-1 if axis == dim else 1 for axis in range(len(dims))])
    return factor_of


def deal_out(rng, own, number, rows, amount, top, bound, lean):
    order = jax.random.permutation(rng, amount)
    heavy_load, common = portions_of(amount, rows * top, bound, lean, True), portions_of(amount, rows * top, bound, lean, False)
    places = jnp.arange(amount)

    def named(tallies, offset_by):
        used = int((tallies > 0).sum())
        fixed = max(1, used // 4)
        shifted = fixed + (places - fixed + offset_by * (used - fixed)) % max(1, amount - fixed)
        return jnp.zeros((amount,), jnp.int32).at[order[jnp.where(places < fixed, places, shifted)]].set(jnp.asarray(tallies, jnp.int32))

    tallies = jnp.where(number % 4 == 0, named(heavy_load, number // 4), named(common, number - number // 4 - 1))
    mixed = jax.random.permutation(jax.random.fold_in(own, 3), amount)
    donor, sink = mixed[0:amount // 2 * 2:2], mixed[1:amount // 2 * 2:2]
    margin = jnp.minimum(tallies[donor] - 1, bound - tallies[sink]) // 2
    margin = jnp.where((donor == order[0]) | (sink == order[0]) | (tallies[sink] == 0), 0, jnp.maximum(margin, 0))
    shifted = jax.random.randint(jax.random.fold_in(own, 4), (amount // 2,), 0, 1 << 20) % (margin + 1)
    tallies = tallies.at[donor].add(-shifted).at[sink].add(shifted)
    items = jnp.searchsorted(jnp.cumsum(tallies), jnp.arange(rows * top), side="right").astype(jnp.int32)
    grid = items.reshape(top, rows).T
    grid = grid[jax.random.permutation(jax.random.fold_in(own, 1), rows)]
    offset_by = jax.random.randint(jax.random.fold_in(own, 2), (rows, 1), 0, top)
    return jnp.take_along_axis(grid, (jnp.arange(top)[None, :] + offset_by) % top, axis=1)


def portions_of(amount, total, most, slope, full):
    loads = [(1 << 20) // math.isqrt(grade ** slope) + 1 for grade in range(1, amount + 1)]
    largest = most if full else min(most, max(-(-total // amount), total * loads[0] // sum(loads)))
    least = 1 if total - largest >= amount - 1 else 0
    holding, rest = [largest] + [least] * (amount - 1), total - largest - least * (amount - 1)
    while rest > 0:
        movable = [i for i in range(1, amount) if holding[i] < largest] or [i for i in range(1, amount) if holding[i] < most]
        mass, budget = sum([loads[i] for i in movable]), rest
        for i in movable:
            more = min(most - holding[i], max(1, budget * loads[i] // mass), rest)
            holding[i] = holding[i] + more
            rest = rest - more
    return np.array(holding)


def centred(rng, dims, width, bound, pieces=(), kind=jnp.bfloat16):
    entries = jax.random.normal(rng, dims, jnp.float32) * width
    if len(pieces) > 0:
        entries = level_of(rng, dims, pieces, -0.22, 0.18) * entries
    return jnp.clip(entries, min=-bound, max=bound).astype(kind)


def setup_inputs(seed: int = 0) -> dict:
    key_list = jax.random.split(jax.random.key(seed), 10)
    tokens = centred(key_list[0], (STEPS, ROWS, D), 1.0, 6.0, ((1, 256),))
    expert_ids_keys = jax.random.split(jax.random.fold_in(key_list[1], 1), STEPS * ROWS // ROW_DEV)
    expert_ids_turns = jax.random.permutation(jax.random.fold_in(key_list[1], 3), STEPS * ROWS // ROW_DEV)
    expert_ids = jax.vmap(lambda own, number: deal_out(jax.random.fold_in(key_list[1], 2), own, number, ROW_DEV, EXPERTS, TOP, CAP, 2))(expert_ids_keys, expert_ids_turns).reshape((STEPS, ROWS, TOP))
    route_gain = jnp.clip(jnp.exp(math.log(1.0) - 2.3025851 * jax.random.uniform(key_list[2], (STEPS, ROWS, TOP), jnp.float32) ** level_of(key_list[2], (STEPS, ROWS, TOP), ((1, 256),), -0.2, 0.2)), 0.1, 1.0)
    gate_up_master = centred(key_list[3], (EXPERTS, D, 2 * FF), D ** -0.5, 0.09375, ((0, 16), (1, 16)), jnp.float32)
    gate_up_moment = centred(key_list[4], (EXPERTS, D, 2 * FF), D ** -0.5, 0.09375, ((0, 16), (1, 16)), jnp.float32)
    gate_up_grad = centred(key_list[5], (EXPERTS, D, 2 * FF), D ** -0.5, 0.09375, ((0, 16), (1, 16)))
    down_master = centred(key_list[6], (EXPERTS, FF, D), FF ** -0.5, 0.21875, ((0, 16), (2, 16)), jnp.float32)
    down_moment = centred(key_list[7], (EXPERTS, FF, D), FF ** -0.5, 0.21875, ((0, 16), (2, 16)), jnp.float32)
    down_grad = centred(key_list[8], (EXPERTS, FF, D), FF ** -0.5, 0.21875, ((0, 16), (2, 16)))
    return dict(tokens=tokens, expert_ids=expert_ids, route_gain=route_gain, gate_up_master=gate_up_master, gate_up_moment=gate_up_moment, gate_up_grad=gate_up_grad, down_master=down_master, down_moment=down_moment, down_grad=down_grad)


def updated(master, moment, grad):
    return (master - 0.5 * (0.8 * moment + 0.2 * grad.astype(jnp.float32))).astype(jnp.bfloat16)


def expert_apply(packed):
    rows_e, gate_up, down = packed
    flat = rows_e.reshape(-1, D)
    projected = jnp.dot(flat, gate_up, preferred_element_type=jnp.float32)
    hidden = (jax.nn.silu(projected[:, :FF]) * projected[:, FF:]).astype(jnp.bfloat16)
    result = jnp.dot(hidden, down, preferred_element_type=jnp.float32).astype(jnp.bfloat16)
    return result.reshape(rows_e.shape)


def reference(tokens, expert_ids, route_gain, gate_up_master, gate_up_moment, gate_up_grad, down_master, down_moment, down_grad):
    gate_up_weight = updated(gate_up_master, gate_up_moment, gate_up_grad)
    down_weight = updated(down_master, down_moment, down_grad)
    blocks = N_ENGINE * N_EXPERT
    flat_ids = expert_ids.reshape(STEPS, blocks, ROW_DEV * TOP)
    picked = (flat_ids[..., None] == jnp.arange(EXPERTS, dtype=jnp.int32)).astype(jnp.int32)
    earlier = jnp.cumsum(picked, axis=2) - picked
    slot_index = jnp.sum(earlier * picked, axis=3).astype(jnp.int32)
    target = (flat_ids * CAP + slot_index).reshape(STEPS, blocks, ROW_DEV, TOP).astype(jnp.int32)
    rows = tokens.reshape(STEPS, blocks, ROW_DEV, D)
    step_index = jnp.arange(STEPS, dtype=jnp.int32)[:, None, None]
    block_index = jnp.arange(blocks, dtype=jnp.int32)[None, :, None]
    buffer = jnp.zeros((STEPS, blocks, EXPERTS * CAP, D), jnp.bfloat16)
    for k in range(TOP):
        buffer = buffer.at[step_index, block_index, target[..., k]].set(rows)
    per_expert = jnp.moveaxis(buffer.reshape(STEPS, blocks, EXPERTS, CAP, D), 2, 0)
    outputs = lax.map(expert_apply, (per_expert, gate_up_weight, down_weight))
    outputs = jnp.moveaxis(outputs, 0, 2).reshape(STEPS, blocks, EXPERTS * CAP, D)
    share = (route_gain / jnp.sum(route_gain, axis=2, keepdims=True)).astype(jnp.bfloat16)
    share = share.reshape(STEPS, blocks, ROW_DEV, TOP)
    total = jnp.zeros((STEPS, blocks, ROW_DEV, D), jnp.float32)
    for k in range(TOP):
        picked_rows = outputs[step_index, block_index, target[..., k]].astype(jnp.float32)
        total = total + share[..., k, None].astype(jnp.float32) * picked_rows
    return total.astype(jnp.bfloat16).reshape(STEPS, ROWS, D)
```

```python
import jax
import jax.numpy as jnp
from jax import lax
from jax.experimental import pallas as pl
from jax.experimental.pallas import tpu as pltpu
from jax.sharding import Mesh, PartitionSpec as P

AXES = ("x", "zl", "core", "zh", "y")
NX, NZL, NC, NZH, NY = 4, 2, 2, 4, 4
MIB = 1 << 20


def updated(master, moment, grad):
    return (master - 0.5 * (0.8 * moment + 0.2 * grad.astype(jnp.float32))).astype(jnp.bfloat16)


def flat(x, zl, c, zh):
    return ((x * NZL + zl) * NC + c) * NZH + zh


def offset_of(x, zl, c):
    return (x + 2 * zl + c) % NZH


def places():
    return [
        (x, zl, c, zh)
        for x in range(NX)
        for zl in range(NZL)
        for c in range(NC)
        for zh in range(NZH)
    ]


SHIFT_Z = [
    (flat(x, zl, c, zh), flat(x, zl, c, (zh + offset_of(x, zl, c)) % NZH))
    for x, zl, c, zh in places()
]
MOVE_X = [
    (flat(x, zl, c, zh), flat((zh - offset_of(x, zl, c)) % NX, zl, c, zh))
    for x, zl, c, zh in places()
]


def ring_index(z):
    return (z % NZL) * NZH + z // NZL


NZ = NZL * NZH
UP = [(ring_index(z), ring_index((z + 1) % NZ)) for z in range(NZ)]
DOWN = [(ring_index(z), ring_index((z - 1) % NZ)) for z in range(NZ)]


def spread(block):
    block = lax.ppermute(block, ("x", "zl", "core", "zh"), SHIFT_Z)
    return lax.ppermute(block, ("x", "zl", "core", "zh"), MOVE_X)


def up(block):
    return lax.ppermute(block, ("zl", "zh"), UP)


def down(block):
    return lax.ppermute(block, ("zl", "zh"), DOWN)


def other_core(block):
    return lax.ppermute(block, "core", [(0, 1), (1, 0)])


def ring(block):
    half = block.shape[0] // 2
    u1, d1 = up(block), down(block)
    u2, d2 = up(u1), down(d1)
    u3, d3 = up(u2), down(d2)
    u4, d4 = up(u3[:half]), down(d3[half:])
    mine = [block, u1, d1, u2, d2, u3, d3, u4, d4]
    return mine + [other_core(piece) for piece in mine]


def shard_table():
    x, zl, c, zh = (lax.axis_index(name) for name in ("x", "zl", "core", "zh"))
    z = NZL * zh + zl
    entries = []
    for core in (c, 1 - c):
        for step in (0, 1, -1, 2, -2, 3, -3, 4):
            at = (z - step + NZ) % NZ
            at_zl, at_zh = at % NZL, at // NZL
            from_x = (at_zh - x - 2 * at_zl - core + 2 * NX) % NX
            entries.append((from_x * NZL + at_zl) * NC + core)
    return jnp.stack(entries).astype(jnp.int32)


def weight_copies(table, pieces, target, sems):
    rows = pieces[0].shape[0]
    half = rows // 2
    copies = []
    for n, piece in enumerate(pieces):
        core, k = divmod(n, 9)
        slot = table[core * 8 + min(k, 7)]
        first = half if k == 8 else 0
        copies.append(
            pltpu.make_async_copy(
                piece, target.at[slot, pl.ds(first, piece.shape[0]), :], sems.at[n]
            )
        )
    return copies


def hidden_kernel(table, x_hbm, *refs):
    pieces, (h_ref, x_buf, w_buf, sems, x_sem) = refs[:18], refs[18:]
    copies = weight_copies(table, pieces, w_buf, sems)
    x_copy = pltpu.make_async_copy(x_hbm, x_buf, x_sem)
    x_copy.start()
    for copy in copies:
        copy.start()
    x_copy.wait()
    for copy in copies:
        copy.wait()
    shards, depth, wide = w_buf.shape
    units = wide // 2
    tile = 256
    for n in range(units // tile):
        w_gate = w_buf[:, :, n * tile : (n + 1) * tile].reshape(shards * depth, tile)
        w_up = w_buf[:, :, units + n * tile : units + (n + 1) * tile].reshape(shards * depth, tile)
        gate = jnp.dot(x_buf[...], w_gate, preferred_element_type=jnp.float32)
        upper = jnp.dot(x_buf[...], w_up, preferred_element_type=jnp.float32)
        h_ref[:, n * tile : (n + 1) * tile] = (gate / (1.0 + jnp.exp(-gate)) * upper).astype(
            h_ref.dtype
        )


def out_kernel(table, h_ref, *refs):
    pieces, (o_ref, w_buf, sems) = refs[:18], refs[18:]
    copies = weight_copies(table, pieces, w_buf, sems)
    for copy in copies:
        copy.start()
    for copy in copies:
        copy.wait()
    shards, _, wide = w_buf.shape
    for s in range(shards):
        o_ref[:, s * wide : (s + 1) * wide] = jnp.dot(
            h_ref[...], w_buf[s], preferred_element_type=jnp.float32
        ).astype(o_ref.dtype)


ANY = pl.BlockSpec(memory_space=pl.ANY)
VMEM = pl.BlockSpec(memory_space=pltpu.VMEM)
SMEM = pl.BlockSpec(memory_space=pltpu.SMEM)


def hidden_of(table, x, pieces):
    rows, wide = x.shape
    depth, cols = pieces[0].shape
    return pl.pallas_call(
        hidden_kernel,
        out_shape=jax.ShapeDtypeStruct((rows, cols // 2), jnp.bfloat16),
        in_specs=[SMEM, ANY] + [ANY] * len(pieces),
        out_specs=VMEM,
        scratch_shapes=[
            pltpu.VMEM((rows, wide), jnp.bfloat16),
            pltpu.VMEM((16, depth, cols), jnp.bfloat16),
            pltpu.SemaphoreType.DMA((len(pieces),)),
            pltpu.SemaphoreType.DMA,
        ],
        compiler_params=pltpu.CompilerParams(vmem_limit_bytes=40 * MIB),
        cost_estimate=pl.CostEstimate(
            flops=2 * rows * wide * cols, bytes_accessed=19 * MIB, transcendentals=rows * cols // 2
        ),
        name="hidden",
    )(table, x, *pieces)


def outputs_of(table, h, pieces):
    rows, units = h.shape
    _, cols = pieces[0].shape
    return pl.pallas_call(
        out_kernel,
        out_shape=jax.ShapeDtypeStruct((rows, 16 * cols), jnp.bfloat16),
        in_specs=[SMEM, VMEM] + [ANY] * len(pieces),
        out_specs=VMEM,
        scratch_shapes=[
            pltpu.VMEM((16, units, cols), jnp.bfloat16),
            pltpu.SemaphoreType.DMA((len(pieces),)),
        ],
        compiler_params=pltpu.CompilerParams(vmem_limit_bytes=30 * MIB),
        cost_estimate=pl.CostEstimate(
            flops=2 * rows * units * cols * 16, bytes_accessed=13 * MIB, transcendentals=0
        ),
        name="expert_out",
    )(table, h, *pieces)


def per_device(
    tokens,
    expert_ids,
    route_gain,
    gate_up_master,
    gate_up_moment,
    gate_up_grad,
    down_master,
    down_moment,
    down_grad,
):
    steps, row_dev, top_k = expert_ids.shape
    width = tokens.shape[2]
    experts = NX * NY
    capacity = 3 * row_dev * top_k // (2 * experts)
    per_expert = steps * capacity
    rows = steps * row_dev
    gate_up_weight = updated(gate_up_master[0], gate_up_moment[0], gate_up_grad[0])
    gate_up_pieces = ring(spread(gate_up_weight))
    down_weight = updated(down_master[0], down_moment[0], down_grad[0])
    down_pieces = ring(spread(down_weight))
    table = shard_table()

    names = expert_ids[..., None] == jnp.arange(experts, dtype=jnp.int32)
    named = jnp.any(names, axis=2).astype(jnp.bfloat16)
    order = jnp.arange(row_dev)
    before = (order[:, None] > order[None, :]).astype(jnp.bfloat16)
    earlier = jnp.einsum("rq,sqe->sre", before, named, preferred_element_type=jnp.float32)
    slot_index = jnp.sum(jnp.where(names, earlier[:, :, None, :], 0.0), axis=3).astype(jnp.int32)
    step_base = capacity * jnp.arange(steps, dtype=jnp.int32)[:, None, None]
    target = (expert_ids * per_expert + step_base + slot_index).reshape(rows, top_k)
    slots = jnp.arange(experts * per_expert, dtype=jnp.int32)
    hits = target[:, None, :] == slots[None, :, None]
    dispatch_table = jnp.any(hits, axis=2).astype(jnp.bfloat16)
    outgoing = jnp.einsum(
        "rp,rd->pd",
        dispatch_table,
        tokens.reshape(rows, width),
        preferred_element_type=jnp.float32,
    ).astype(jnp.bfloat16)
    received = lax.all_to_all(outgoing, ("x", "y"), split_axis=0, concat_axis=0, tiled=True)

    hidden = hidden_of(table, received, gate_up_pieces)
    expert_out = outputs_of(table, hidden, down_pieces)

    returned = lax.all_to_all(expert_out, ("x", "y"), split_axis=0, concat_axis=0, tiled=True)
    share = (route_gain / jnp.sum(route_gain, axis=2, keepdims=True)).astype(jnp.bfloat16)
    share = share.reshape(rows, 1, top_k)
    combine_table = jnp.sum(
        jnp.where(hits, share.astype(jnp.float32), 0.0), axis=2
    ).astype(jnp.bfloat16)
    mixed = jnp.dot(combine_table, returned, preferred_element_type=jnp.float32)
    return mixed.astype(jnp.bfloat16).reshape(steps, row_dev, width)


def solution(mesh):
    grid = Mesh(mesh.devices.reshape(NX, NZL, NC, NZH, NY), AXES)
    engine, expert = ("x", "zl", "core"), ("zh", "y")
    rows = P(None, AXES, None)
    return jax.shard_map(
        per_device,
        mesh=grid,
        in_specs=(
            rows,
            rows,
            rows,
            P(expert, engine, None),
            P(expert, engine, None),
            P(expert, engine, None),
            P(expert, None, engine),
            P(expert, None, engine),
            P(expert, None, engine),
        ),
        out_specs=rows,
        check_vma=False,
    )
```

```python
import jax
import jax.numpy as jnp
import numpy as np
from jax import lax
from jax.experimental import pallas as pl
from jax.experimental.pallas import tpu as pltpu
from jax.sharding import Mesh, PartitionSpec as P

AXES = ("x", "zl", "core", "zh", "y")
NX, NZL, NC, NZH, NY = 4, 2, 2, 4, 4
MIB = 1 << 20


def updated(master, moment, grad):
    return (master - 0.5 * (0.8 * moment + 0.2 * grad.astype(jnp.float32))).astype(jnp.bfloat16)


def flat(x, zl, c, zh):
    return ((x * NZL + zl) * NC + c) * NZH + zh


def places():
    return [
        (x, zl, c, zh)
        for x in range(NX)
        for zl in range(NZL)
        for c in range(NC)
        for zh in range(NZH)
    ]


NZ = NZL * NZH


def host_of(x, zl, c, zh):
    hops = x if c == 0 else NX - 1 - x
    z = (NZL * zh + 1 + hops) % NZ if zl else (NZL * zh - hops) % NZ
    return zh, z % NZL, c, z // NZL


SPREAD = [(flat(*place), flat(*host_of(*place))) for place in places()]
SHARD_AT = {
    host_of(x, zl, c, zh): (x * NZL + zl) * NC + c for x, zl, c, zh in places()
}


def ring_index(z, c):
    return (z % NZL * NC + c) * NZH + z // NZL


def ring_step(z, c):
    return (z + 1 - 2 * c) % NZ


PASS_ON = [(ring_index(z, c), ring_index(ring_step(z, c), c)) for z in range(NZ) for c in range(NC)]


def spread(block):
    return lax.ppermute(block, ("x", "zl", "core", "zh"), SPREAD)


def pass_on(block):
    return lax.ppermute(block, ("zl", "core", "zh"), PASS_ON)


def after(value, *others):
    return lax.optimization_barrier((value,) + others)[0]


def other_core(block):
    return lax.ppermute(block, "core", [(0, 1), (1, 0)])


def ring(block):
    mine = [block]
    for _ in range(NZ - 1):
        mine.append(pass_on(mine[-1]))
    return mine + [other_core(piece) for piece in mine]


def shards_at(x, zl, c, zh):
    z = NZL * zh + zl
    entries = []
    for core in (c, 1 - c):
        for step in range(NZ):
            at = (z - step * (1 - 2 * core)) % NZ
            entries.append(SHARD_AT[x, at % NZL, core, at // NZL])
    return entries


SHARDS = np.array([shards_at(*place) for place in places()], np.int32)


def shard_table():
    x, zl, c, zh = (lax.axis_index(name) for name in ("x", "zl", "core", "zh"))
    return lax.dynamic_index_in_dim(jnp.asarray(SHARDS), flat(x, zl, c, zh), keepdims=False)


def hidden_kernel(table, x_hbm, *refs):
    pieces, (h_ref, x_buf, w_buf, sems, x_sem) = refs[:16], refs[16:]
    copies = [
        pltpu.make_async_copy(piece, w_buf.at[table[n]], sems.at[n])
        for n, piece in enumerate(pieces)
    ]
    x_copy = pltpu.make_async_copy(x_hbm, x_buf, x_sem)
    x_copy.start()
    for copy in copies:
        copy.start()
    x_copy.wait()
    for copy in copies:
        copy.wait()
    shards, depth, wide = w_buf.shape
    units = wide // 2
    tile = 256

    def columns(n, carry):
        first = pl.multiple_of(n * tile, tile)
        w_gate = w_buf[:, :, pl.ds(first, tile)].reshape(shards * depth, tile)
        w_up = w_buf[:, :, pl.ds(units + first, tile)].reshape(shards * depth, tile)
        gate = jnp.dot(x_buf[...], w_gate, preferred_element_type=jnp.float32)
        upper = jnp.dot(x_buf[...], w_up, preferred_element_type=jnp.float32)
        h_ref[:, pl.ds(first, tile)] = (gate / (1.0 + jnp.exp(-gate)) * upper).astype(h_ref.dtype)
        return carry

    lax.fori_loop(0, units // tile, columns, 0)


def out_kernel(table, h_ref, *refs):
    pieces, (o_ref, w_buf, sems) = refs[:16], refs[16:]
    wide = pieces[0].shape[1]
    copies = [
        pltpu.make_async_copy(
            piece, w_buf.at[:, pl.ds(pl.multiple_of(table[n] * wide, wide), wide)], sems.at[n]
        )
        for n, piece in enumerate(pieces)
    ]
    for copy in copies:
        copy.start()
    for copy in copies:
        copy.wait()
    tile = 1024

    def columns(n, carry):
        at = pl.ds(pl.multiple_of(n * tile, tile), tile)
        o_ref[:, at] = jnp.dot(
            h_ref[...], w_buf[:, at], preferred_element_type=jnp.float32
        ).astype(o_ref.dtype)
        return carry

    lax.fori_loop(0, w_buf.shape[1] // tile, columns, 0)


ANY = pl.BlockSpec(memory_space=pl.ANY)
VMEM = pl.BlockSpec(memory_space=pltpu.VMEM)
SMEM = pl.BlockSpec(memory_space=pltpu.SMEM)


def hidden_of(table, x, pieces):
    rows, wide = x.shape
    depth, cols = pieces[0].shape
    return pl.pallas_call(
        hidden_kernel,
        out_shape=jax.ShapeDtypeStruct((rows, cols // 2), jnp.bfloat16),
        in_specs=[SMEM, ANY] + [ANY] * len(pieces),
        out_specs=VMEM,
        scratch_shapes=[
            pltpu.VMEM((rows, wide), jnp.bfloat16),
            pltpu.VMEM((16, depth, cols), jnp.bfloat16),
            pltpu.SemaphoreType.DMA((len(pieces),)),
            pltpu.SemaphoreType.DMA,
        ],
        compiler_params=pltpu.CompilerParams(vmem_limit_bytes=22 * MIB),
        cost_estimate=pl.CostEstimate(
            flops=2 * rows * wide * cols, bytes_accessed=19 * MIB, transcendentals=rows * cols // 2
        ),
        name="hidden",
    )(table, x, *pieces)


def outputs_of(table, h, pieces):
    rows, units = h.shape
    _, cols = pieces[0].shape
    return pl.pallas_call(
        out_kernel,
        out_shape=jax.ShapeDtypeStruct((rows, 16 * cols), jnp.bfloat16),
        in_specs=[SMEM, VMEM] + [ANY] * len(pieces),
        out_specs=VMEM,
        scratch_shapes=[
            pltpu.VMEM((units, 16 * cols), jnp.bfloat16),
            pltpu.SemaphoreType.DMA((len(pieces),)),
        ],
        compiler_params=pltpu.CompilerParams(vmem_limit_bytes=16 * MIB),
        cost_estimate=pl.CostEstimate(
            flops=2 * rows * units * cols * 16, bytes_accessed=13 * MIB, transcendentals=0
        ),
        name="expert_out",
    )(table, h, *pieces)


def per_device(
    tokens,
    expert_ids,
    route_gain,
    gate_up_master,
    gate_up_moment,
    gate_up_grad,
    down_master,
    down_moment,
    down_grad,
):
    steps, row_dev, top_k = expert_ids.shape
    width = tokens.shape[2]
    experts = NX * NY
    capacity = 3 * row_dev * top_k // (2 * experts)
    gate_up_weight = updated(gate_up_master[0], gate_up_moment[0], gate_up_grad[0])
    down_weight = updated(down_master[0], down_moment[0], down_grad[0])
    gate_up_block = spread(gate_up_weight)
    down_block = spread(down_weight)
    gate_up_pieces = ring(gate_up_block)
    down_pieces = ring(down_block)
    table = shard_table()

    names = expert_ids[..., None] == jnp.arange(experts, dtype=jnp.int32)
    named = jnp.any(names, axis=2).astype(jnp.bfloat16)
    order = jnp.arange(row_dev)
    before = (order[:, None] > order[None, :]).astype(jnp.bfloat16)
    earlier = jnp.einsum("rq,sqe->sre", before, named, preferred_element_type=jnp.float32)
    slot_index = jnp.sum(jnp.where(names, earlier[:, :, None, :], 0.0), axis=3).astype(jnp.int32)
    target = expert_ids * capacity + slot_index
    slots = jnp.arange(experts * capacity, dtype=jnp.int32)
    hits = target[:, :, None, :] == slots[None, None, :, None]
    dispatch_table = jnp.any(hits, axis=3).astype(jnp.bfloat16)
    share = (route_gain / jnp.sum(route_gain, axis=2, keepdims=True)).astype(jnp.bfloat16)
    combine_table = jnp.sum(
        jnp.where(hits, share[:, :, None, :].astype(jnp.float32), 0.0), axis=3
    ).astype(jnp.bfloat16)

    gate = (gate_up_block, down_block)
    mixed = []
    received = []
    for s in range(steps):
        outgoing = jnp.einsum(
            "rp,rd->pd", dispatch_table[s], tokens[s], preferred_element_type=jnp.float32
        ).astype(jnp.bfloat16)
        arrived = lax.all_to_all(
            after(outgoing, *gate), ("x", "y"), split_axis=0, concat_axis=0, tiled=True
        )
        received.append(arrived)
        gate = (arrived, gate_up_pieces[3])
    hiddens = [hidden_of(table, block, gate_up_pieces) for block in received]
    for s in range(steps):
        expert_out = outputs_of(table, hiddens[s], down_pieces)
        returned = lax.all_to_all(expert_out, ("x", "y"), split_axis=0, concat_axis=0, tiled=True)
        mixed.append(
            jnp.dot(combine_table[s], returned, preferred_element_type=jnp.float32).astype(
                jnp.bfloat16
            )
        )
    return jnp.stack(mixed)


def solution(mesh):
    grid = Mesh(mesh.devices.reshape(NX, NZL, NC, NZH, NY), AXES)
    engine, expert = ("x", "zl", "core"), ("zh", "y")
    rows = P(None, AXES, None)
    return jax.shard_map(
        per_device,
        mesh=grid,
        in_specs=(
            rows,
            rows,
            rows,
            P(expert, engine, None),
            P(expert, engine, None),
            P(expert, engine, None),
            P(expert, None, engine),
            P(expert, None, engine),
            P(expert, None, engine),
        ),
        out_specs=rows,
        check_vma=False,
    )
```

```python
import jax
import jax.numpy as jnp
import numpy as np
from jax import lax
from jax.experimental import pallas as pl
from jax.experimental.pallas import tpu as pltpu
from jax.sharding import Mesh, PartitionSpec as P

AXES = ("x", "zl", "core", "zh", "y")
NX, NZL, NC, NZH, NY = 4, 2, 2, 4, 4
MIB = 1 << 20
TILE = 256
OUT_TILE = 1024
CUT = 1152


def updated(master, moment, grad):
    return (master - 0.5 * (0.8 * moment + 0.2 * grad.astype(jnp.float32))).astype(jnp.bfloat16)


def flat(x, zl, c, zh):
    return ((x * NZL + zl) * NC + c) * NZH + zh


def places():
    return [
        (x, zl, c, zh)
        for x in range(NX)
        for zl in range(NZL)
        for c in range(NC)
        for zh in range(NZH)
    ]


NZ = NZL * NZH


def host_of(x, zl, c, zh):
    hops = x if c == 0 else NX - 1 - x
    z = (NZL * zh + 1 + hops) % NZ if zl else (NZL * zh - hops) % NZ
    return zh, z % NZL, c, z // NZL


SPREAD = [(flat(*place), flat(*host_of(*place))) for place in places()]
SHARD_AT = {
    host_of(x, zl, c, zh): (x * NZL + zl) * NC + c for x, zl, c, zh in places()
}


def ring_index(z, c):
    return (z % NZL * NC + c) * NZH + z // NZL


def ring_step(z, c):
    return (z + 1 - 2 * c) % NZ


PASS_ON = [(ring_index(z, c), ring_index(ring_step(z, c), c)) for z in range(NZ) for c in range(NC)]


def in_hbm(value):
    return pltpu.with_memory_space_constraint(value, pltpu.HBM)


def spread(block):
    return in_hbm(lax.ppermute(block, ("x", "zl", "core", "zh"), SPREAD))


def pass_on(block):
    return in_hbm(lax.ppermute(block, ("zl", "core", "zh"), PASS_ON))


def other_core(block):
    return in_hbm(lax.ppermute(block, "core", [(0, 1), (1, 0)]))


def after(value, *others):
    return lax.optimization_barrier((value,) + others)[0]


def rings(first, second, ready):
    mine, others = ([first], [second]), ([], [])
    for step in range(NZ):
        for stream in (0, 1):
            others[stream].append(other_core(mine[stream][step]))
        if step == NZ - 1:
            break
        for stream in (0, 1):
            block = mine[stream][step]
            if step:
                block = after(block, mine[1 - stream][step - 1], others[stream][step - 1])
            else:
                block = after(block, *ready)
            mine[stream].append(pass_on(block))
    return [mine[stream] + others[stream] for stream in (0, 1)]


def shards_at(x, zl, c, zh):
    z = NZL * zh + zl
    entries = []
    for core in (c, 1 - c):
        for step in range(NZ):
            at = (z - step * (1 - 2 * core)) % NZ
            entries.append(SHARD_AT[x, at % NZL, core, at // NZL])
    return entries


SHARDS = np.array([shards_at(*place) for place in places()], np.int32)


def shard_table():
    x, zl, c, zh = (lax.axis_index(name) for name in ("x", "zl", "core", "zh"))
    return lax.dynamic_index_in_dim(jnp.asarray(SHARDS), flat(x, zl, c, zh), keepdims=False)


def first_kernel(master, moment, grad, o_ref):
    o_ref[...] = packed(master, moment, grad, 0, o_ref.shape[1])


def second_kernel(master, moment, grad, down_master, down_moment, down_grad, o_ref):
    depth, wide = master.shape
    o_ref[:, : wide - CUT] = packed(master, moment, grad, CUT, wide)
    for j in range(down_master.shape[0] // depth):
        rows = pl.ds(j * depth, depth)
        o_ref[:, wide - CUT + j * depth : wide - CUT + (j + 1) * depth] = updated(
            down_master[rows, :], down_moment[rows, :], down_grad[rows, :]
        )


def packed(master, moment, grad, low, high):
    units = master.shape[1] // 2
    parts = []
    for n in range(units // TILE):
        for first in (n * TILE, units + n * TILE):
            at = len(parts) * TILE
            begin, end = max(low, at), min(high, at + TILE)
            parts.append(None)
            if begin < end:
                cols = pl.ds(first + begin - at, end - begin)
                parts[-1] = updated(master[:, cols], moment[:, cols], grad[:, cols])
    return jnp.concatenate([part for part in parts if part is not None], axis=1)


def first_block(gate_up):
    return pl.pallas_call(
        first_kernel,
        out_shape=jax.ShapeDtypeStruct((gate_up[0].shape[0], CUT), jnp.bfloat16),
        name="first_block",
    )(*gate_up)


def second_block(gate_up, down):
    return pl.pallas_call(
        second_kernel,
        out_shape=jax.ShapeDtypeStruct((gate_up[0].shape[0], CUT), jnp.bfloat16),
        name="second_block",
    )(*gate_up, *down)


def expert_kernel(table, x_hbm, *refs):
    firsts, seconds = refs[:16], refs[16:32]
    o_hbm, x_buf, up_buf, down_buf, o_buf, up_sems, down_sems, x_sem, o_sems = refs[32:]
    shards, depth, wide = up_buf.shape
    units = wide // 2
    blocks = units // depth
    tiles = units // TILE
    rest = wide - CUT
    x_copy = pltpu.make_async_copy(x_hbm, x_buf, x_sem)
    x_copy.start()
    up_copies = [[] for _ in range(tiles)]
    down_copies = []
    for n, (first, second) in enumerate(zip(firsts, seconds)):
        slot = table[n]

        def copy_columns(source, low, high, target, m):
            return pltpu.make_async_copy(
                source.at[:, pl.ds(low, high - low)],
                up_buf.at[slot, :, pl.ds(target, high - low)],
                up_sems.at[(tiles + 1) * n + m],
            )

        for m in range(tiles):
            low, high = 2 * TILE * m, 2 * TILE * (m + 1)
            if low < CUT:
                up_copies[m].append(copy_columns(first, low, min(high, CUT), low, m))
            if high > CUT:
                up_copies[m].append(copy_columns(second, 0, rest, CUT, tiles))
        at = pl.ds(pl.multiple_of(slot * depth, depth), depth)
        down_copies += [
            pltpu.make_async_copy(
                second.at[:, pl.ds(rest + j * depth, depth)],
                down_buf.at[pl.ds(j * depth, depth), at],
                down_sems.at[blocks * n + j],
            )
            for j in range(blocks)
        ]
    for copies in up_copies:
        for copy in copies:
            copy.start()
    for copy in down_copies:
        copy.start()
    x_copy.wait()
    hidden = []
    for m in range(tiles):
        for copy in up_copies[m]:
            copy.wait()
        weight = up_buf[:, :, 2 * TILE * m : 2 * TILE * (m + 1)].reshape(shards * depth, 2 * TILE)
        both = jnp.dot(x_buf[...], weight, preferred_element_type=jnp.float32)
        gate, upper = both[:, :TILE], both[:, TILE:]
        hidden.append((gate / (1.0 + jnp.exp(-gate)) * upper).astype(jnp.bfloat16))
    hidden = jnp.concatenate(hidden, axis=1)
    for copy in down_copies:
        copy.wait()

    def out_copy(n):
        at = pl.ds(pl.multiple_of(n * OUT_TILE, OUT_TILE), OUT_TILE)
        return pltpu.make_async_copy(o_buf.at[:, at], o_hbm.at[:, at], o_sems.at[n])

    def columns(n, carry):
        at = pl.ds(pl.multiple_of(n * OUT_TILE, OUT_TILE), OUT_TILE)
        o_buf[:, at] = jnp.dot(
            hidden, down_buf[:, at], preferred_element_type=jnp.float32
        ).astype(o_buf.dtype)
        out_copy(n).start()
        return carry

    out_tiles = down_buf.shape[1] // OUT_TILE
    lax.fori_loop(0, out_tiles, columns, 0)
    for n in range(out_tiles):
        out_copy(n).wait()


HBM = pl.BlockSpec(memory_space=pltpu.HBM)
VMEM = pl.BlockSpec(memory_space=pltpu.VMEM)
SMEM = pl.BlockSpec(memory_space=pltpu.SMEM)


def experts_of(table, x, firsts, seconds, units):
    rows, width = x.shape
    depth = firsts[0].shape[0]
    return pl.pallas_call(
        expert_kernel,
        out_shape=jax.ShapeDtypeStruct((rows, width), jnp.bfloat16),
        in_specs=[SMEM, HBM] + [HBM] * 32,
        out_specs=HBM,
        scratch_shapes=[
            pltpu.VMEM((rows, width), jnp.bfloat16),
            pltpu.VMEM((16, depth, 2 * units), jnp.bfloat16),
            pltpu.VMEM((units, width), jnp.bfloat16),
            pltpu.VMEM((rows, width), jnp.bfloat16),
            pltpu.SemaphoreType.DMA((16 * (units // TILE + 1),)),
            pltpu.SemaphoreType.DMA((16 * (units // depth),)),
            pltpu.SemaphoreType.DMA,
            pltpu.SemaphoreType.DMA((width // OUT_TILE,)),
        ],
        compiler_params=pltpu.CompilerParams(vmem_limit_bytes=40 * MIB),
        cost_estimate=pl.CostEstimate(
            flops=6 * rows * width * units,
            bytes_accessed=24 * MIB,
            transcendentals=rows * units,
        ),
        name="experts",
    )(table, x, *firsts, *seconds)


def per_device(
    tokens,
    expert_ids,
    route_gain,
    gate_up_master,
    gate_up_moment,
    gate_up_grad,
    down_master,
    down_moment,
    down_grad,
):
    steps, row_dev, top_k = expert_ids.shape
    width = tokens.shape[2]
    experts = NX * NY
    capacity = 3 * row_dev * top_k // (2 * experts)
    units = down_master.shape[1]
    gate_up = (gate_up_master[0], gate_up_moment[0], gate_up_grad[0])
    down = (down_master[0], down_moment[0], down_grad[0])
    packed_first = first_block(gate_up)
    first = spread(packed_first)
    table = shard_table()

    names = expert_ids[..., None] == jnp.arange(experts, dtype=jnp.int32)
    named = jnp.any(names, axis=2).astype(jnp.bfloat16)
    order = jnp.arange(row_dev)
    before = (order[:, None] > order[None, :]).astype(jnp.bfloat16)
    earlier = jnp.einsum("rq,sqe->sre", before, named, preferred_element_type=jnp.float32)
    slot_index = jnp.sum(jnp.where(names, earlier[:, :, None, :], 0.0), axis=3).astype(jnp.int32)
    target = expert_ids * capacity + slot_index
    slots = jnp.arange(experts * capacity, dtype=jnp.int32)
    hits = target[:, :, None, :] == slots[None, None, :, None]
    dispatch_table = jnp.any(hits, axis=3).astype(jnp.bfloat16)
    share = (route_gain / jnp.sum(route_gain, axis=2, keepdims=True)).astype(jnp.bfloat16)
    combine_table = jnp.sum(
        jnp.where(hits, share[:, :, None, :].astype(jnp.float32), 0.0), axis=3
    ).astype(jnp.bfloat16)

    outgoing = [
        jnp.einsum(
            "rp,rd->pd", dispatch_table[s], tokens[s], preferred_element_type=jnp.float32
        ).astype(jnp.bfloat16)
        for s in range(steps)
    ]
    packed_second = second_block(gate_up, down)
    second = spread(packed_second)
    firsts, seconds = rings(first, second, outgoing)
    gate = (packed_first, packed_second)
    mixed = []
    received = []
    for s in range(steps):
        arrived = lax.all_to_all(
            after(outgoing[s], *gate), ("x", "y"), split_axis=0, concat_axis=0, tiled=True
        )
        received.append(arrived)
        gate = (arrived, firsts[1], seconds[1])
    for s in range(steps):
        expert_out = experts_of(table, received[s], firsts, seconds, units)
        returned = lax.all_to_all(expert_out, ("x", "y"), split_axis=0, concat_axis=0, tiled=True)
        mixed.append(
            jnp.dot(combine_table[s], returned, preferred_element_type=jnp.float32).astype(
                jnp.bfloat16
            )
        )
    return jnp.stack(mixed)


def solution(mesh):
    grid = Mesh(mesh.devices.reshape(NX, NZL, NC, NZH, NY), AXES)
    engine, expert = ("x", "zl", "core"), ("zh", "y")
    rows = P(None, AXES, None)
    return jax.shard_map(
        per_device,
        mesh=grid,
        in_specs=(
            rows,
            rows,
            rows,
            P(expert, engine, None),
            P(expert, engine, None),
            P(expert, engine, None),
            P(expert, None, engine),
            P(expert, None, engine),
            P(expert, None, engine),
        ),
        out_specs=rows,
        check_vma=False,
    )
```

```python
import jax
import jax.numpy as jnp
import numpy as np
from jax import lax
from jax.experimental import pallas as pl
from jax.experimental.pallas import tpu as pltpu
from jax.sharding import Mesh, PartitionSpec as P

AXES = ("x", "zl", "core", "zh", "y")
NX, NZL, NC, NZH, NY = 4, 2, 2, 4, 4
MIB = 1 << 20
TILE = 256
OUT_TILE = 1024
CUT = 1152


def updated(master, moment, grad):
    return (master - 0.5 * (0.8 * moment + 0.2 * grad.astype(jnp.float32))).astype(jnp.bfloat16)


def flat(x, zl, c, zh):
    return ((x * NZL + zl) * NC + c) * NZH + zh


def places():
    return [
        (x, zl, c, zh)
        for x in range(NX)
        for zl in range(NZL)
        for c in range(NC)
        for zh in range(NZH)
    ]


NZ = NZL * NZH


def host_of(x, zl, c, zh):
    hops = x if c == 0 else NX - 1 - x
    z = (NZL * zh + 1 + hops) % NZ if zl else (NZL * zh - hops) % NZ
    return zh, z % NZL, c, z // NZL


SPREAD = [(flat(*place), flat(*host_of(*place))) for place in places()]
SHARD_AT = {
    host_of(x, zl, c, zh): (x * NZL + zl) * NC + c for x, zl, c, zh in places()
}


def ring_index(z, c):
    return (z % NZL * NC + c) * NZH + z // NZL


def ring_step(z, c):
    return (z + 1 - 2 * c) % NZ


PASS_ON = [(ring_index(z, c), ring_index(ring_step(z, c), c)) for z in range(NZ) for c in range(NC)]


def in_hbm(value):
    return pltpu.with_memory_space_constraint(value, pltpu.HBM)


def spread(block):
    return in_hbm(lax.ppermute(block, ("x", "zl", "core", "zh"), SPREAD))


def pass_on(block):
    return in_hbm(lax.ppermute(block, ("zl", "core", "zh"), PASS_ON))


def other_core(block):
    return in_hbm(lax.ppermute(block, "core", [(0, 1), (1, 0)]))


def after(value, *others):
    return lax.optimization_barrier((value,) + others)[0]


def rings(first, second, ready):
    mine, others = ([first], [second]), ([], [])
    for step in range(NZ):
        for stream in (0, 1):
            others[stream].append(other_core(mine[stream][step]))
        if step == NZ - 1:
            break
        for stream in (0, 1):
            block = mine[stream][step]
            if step:
                block = after(block, mine[1 - stream][step - 1], others[stream][step - 1])
            else:
                block = after(block, *ready)
            mine[stream].append(pass_on(block))
    return [mine[stream] + others[stream] for stream in (0, 1)]


def shards_at(x, zl, c, zh):
    z = NZL * zh + zl
    entries = []
    for core in (c, 1 - c):
        for step in range(NZ):
            at = (z - step * (1 - 2 * core)) % NZ
            entries.append(SHARD_AT[x, at % NZL, core, at // NZL])
    return entries


SHARDS = np.array([shards_at(*place) for place in places()], np.int32)


def shard_table():
    x, zl, c, zh = (lax.axis_index(name) for name in ("x", "zl", "core", "zh"))
    return lax.dynamic_index_in_dim(jnp.asarray(SHARDS), flat(x, zl, c, zh), keepdims=False)


def first_kernel(master, moment, grad, o_ref):
    o_ref[...] = packed(master, moment, grad, 0, o_ref.shape[1])


def second_kernel(master, moment, grad, down_master, down_moment, down_grad, o_ref):
    depth, wide = master.shape
    o_ref[:, : wide - CUT] = packed(master, moment, grad, CUT, wide)
    for j in range(down_master.shape[0] // depth):
        rows = pl.ds(j * depth, depth)
        o_ref[:, wide - CUT + j * depth : wide - CUT + (j + 1) * depth] = updated(
            down_master[rows, :], down_moment[rows, :], down_grad[rows, :]
        )


def packed(master, moment, grad, low, high):
    units = master.shape[1] // 2
    parts = []
    for n in range(units // TILE):
        for first in (n * TILE, units + n * TILE):
            at = len(parts) * TILE
            begin, end = max(low, at), min(high, at + TILE)
            parts.append(None)
            if begin < end:
                cols = pl.ds(first + begin - at, end - begin)
                parts[-1] = updated(master[:, cols], moment[:, cols], grad[:, cols])
    return jnp.concatenate([part for part in parts if part is not None], axis=1)


def first_block(gate_up):
    return pl.pallas_call(
        first_kernel,
        out_shape=jax.ShapeDtypeStruct((gate_up[0].shape[0], CUT), jnp.bfloat16),
        name="first_block",
    )(*gate_up)


def second_block(gate_up, down):
    return pl.pallas_call(
        second_kernel,
        out_shape=jax.ShapeDtypeStruct((gate_up[0].shape[0], CUT), jnp.bfloat16),
        name="second_block",
    )(*gate_up, *down)


def expert_kernel(table, x_hbm, *refs):
    firsts, seconds = refs[:16], refs[16:32]
    o_hbm, x_buf, up_buf, down_buf, o_buf, up_sems, down_sems, x_sem, o_sems = refs[32:]
    shards, depth, wide = up_buf.shape
    units = wide // 2
    blocks = units // depth
    tiles = units // TILE
    rest = wide - CUT
    x_copy = pltpu.make_async_copy(x_hbm, x_buf, x_sem)
    x_copy.start()
    up_copies = [[] for _ in range(tiles)]
    down_copies = []
    for n, (first, second) in enumerate(zip(firsts, seconds)):
        slot = table[n]

        def copy_columns(source, low, high, target, m):
            return pltpu.make_async_copy(
                source.at[:, pl.ds(low, high - low)],
                up_buf.at[slot, :, pl.ds(target, high - low)],
                up_sems.at[(tiles + 1) * n + m],
            )

        for m in range(tiles):
            low, high = 2 * TILE * m, 2 * TILE * (m + 1)
            if low < CUT:
                up_copies[m].append(copy_columns(first, low, min(high, CUT), low, m))
            if high > CUT:
                up_copies[m].append(copy_columns(second, 0, rest, CUT, tiles))
        at = pl.ds(pl.multiple_of(slot * depth, depth), depth)
        down_copies += [
            pltpu.make_async_copy(
                second.at[:, pl.ds(rest + j * depth, depth)],
                down_buf.at[pl.ds(j * depth, depth), at],
                down_sems.at[blocks * n + j],
            )
            for j in range(blocks)
        ]
    for copies in up_copies:
        for copy in copies:
            copy.start()
    for copy in down_copies:
        copy.start()
    x_copy.wait()
    hidden = []
    for m in range(tiles):
        for copy in up_copies[m]:
            copy.wait()
        weight = up_buf[:, :, 2 * TILE * m : 2 * TILE * (m + 1)].reshape(shards * depth, 2 * TILE)
        both = jnp.dot(x_buf[...], weight, preferred_element_type=jnp.float32)
        gate, upper = both[:, :TILE], both[:, TILE:]
        hidden.append((gate / (1.0 + jnp.exp(-gate)) * upper).astype(jnp.bfloat16))
    hidden = jnp.concatenate(hidden, axis=1)
    for copy in down_copies:
        copy.wait()

    def out_copy(n):
        at = pl.ds(pl.multiple_of(n * OUT_TILE, OUT_TILE), OUT_TILE)
        return pltpu.make_async_copy(o_buf.at[:, at], o_hbm.at[:, at], o_sems.at[n])

    def columns(n, carry):
        at = pl.ds(pl.multiple_of(n * OUT_TILE, OUT_TILE), OUT_TILE)
        o_buf[:, at] = jnp.dot(
            hidden, down_buf[:, at], preferred_element_type=jnp.float32
        ).astype(o_buf.dtype)
        out_copy(n).start()
        return carry

    out_tiles = down_buf.shape[1] // OUT_TILE
    lax.fori_loop(0, out_tiles, columns, 0)
    for n in range(out_tiles):
        out_copy(n).wait()


HBM = pl.BlockSpec(memory_space=pltpu.HBM)
VMEM = pl.BlockSpec(memory_space=pltpu.VMEM)
SMEM = pl.BlockSpec(memory_space=pltpu.SMEM)


def experts_of(table, x, firsts, seconds, units):
    rows, width = x.shape
    depth = firsts[0].shape[0]
    return pl.pallas_call(
        expert_kernel,
        out_shape=pltpu.HBM((rows, width), jnp.bfloat16),
        in_specs=[SMEM, HBM] + [HBM] * 32,
        out_specs=HBM,
        scratch_shapes=[
            pltpu.VMEM((rows, width), jnp.bfloat16),
            pltpu.VMEM((16, depth, 2 * units), jnp.bfloat16),
            pltpu.VMEM((units, width), jnp.bfloat16),
            pltpu.VMEM((rows, width), jnp.bfloat16),
            pltpu.SemaphoreType.DMA((16 * (units // TILE + 1),)),
            pltpu.SemaphoreType.DMA((16 * (units // depth),)),
            pltpu.SemaphoreType.DMA,
            pltpu.SemaphoreType.DMA((width // OUT_TILE,)),
        ],
        compiler_params=pltpu.CompilerParams(vmem_limit_bytes=40 * MIB),
        cost_estimate=pl.CostEstimate(
            flops=6 * rows * width * units,
            bytes_accessed=24 * MIB,
            transcendentals=rows * units,
        ),
        name="experts",
    )(table, x, *firsts, *seconds)


def per_device(
    tokens,
    expert_ids,
    route_gain,
    gate_up_master,
    gate_up_moment,
    gate_up_grad,
    down_master,
    down_moment,
    down_grad,
):
    steps, row_dev, top_k = expert_ids.shape
    width = tokens.shape[2]
    experts = NX * NY
    capacity = 3 * row_dev * top_k // (2 * experts)
    units = down_master.shape[1]
    gate_up = (gate_up_master[0], gate_up_moment[0], gate_up_grad[0])
    down = (down_master[0], down_moment[0], down_grad[0])
    packed_first = first_block(gate_up)
    first = spread(packed_first)
    table = shard_table()

    names = expert_ids[..., None] == jnp.arange(experts, dtype=jnp.int32)
    named = jnp.any(names, axis=2).astype(jnp.bfloat16)
    order = jnp.arange(row_dev)
    before = (order[:, None] > order[None, :]).astype(jnp.bfloat16)
    earlier = jnp.einsum("rq,sqe->sre", before, named, preferred_element_type=jnp.float32)
    slot_index = jnp.sum(jnp.where(names, earlier[:, :, None, :], 0.0), axis=3).astype(jnp.int32)
    target = expert_ids * capacity + slot_index
    slots = jnp.arange(experts * capacity, dtype=jnp.int32)
    hits = target[:, :, None, :] == slots[None, None, :, None]
    dispatch_table = jnp.any(hits, axis=3).astype(jnp.bfloat16)
    share = (route_gain / jnp.sum(route_gain, axis=2, keepdims=True)).astype(jnp.bfloat16)
    combine_table = jnp.sum(
        jnp.where(hits, share[:, :, None, :].astype(jnp.float32), 0.0), axis=3
    ).astype(jnp.bfloat16)

    outgoing = [
        jnp.einsum(
            "rp,rd->pd", dispatch_table[s], tokens[s], preferred_element_type=jnp.float32
        ).astype(jnp.bfloat16)
        for s in range(steps)
    ]
    packed_second = second_block(gate_up, down)
    second = spread(packed_second)
    firsts, seconds = rings(first, second, outgoing)
    gate = (packed_first, packed_second)
    mixed = jnp.zeros((steps, row_dev, width), jnp.bfloat16)
    received = []
    for s in range(steps):
        arrived = lax.all_to_all(
            after(outgoing[s], *gate), ("x", "y"), split_axis=0, concat_axis=0, tiled=True
        )
        received.append(arrived)
        gate = (arrived, firsts[1], seconds[1])
    for s in range(steps):
        expert_out = experts_of(table, received[s], firsts, seconds, units)
        returned = lax.all_to_all(expert_out, ("x", "y"), split_axis=0, concat_axis=0, tiled=True)
        returned = pltpu.with_memory_space_constraint(returned, pl.ANY)
        part = jnp.dot(combine_table[s], returned, preferred_element_type=jnp.float32)
        mixed = lax.dynamic_update_slice(
            after(mixed), part.astype(jnp.bfloat16)[None], (s, 0, 0)
        )
    return mixed


def solution(mesh):
    grid = Mesh(mesh.devices.reshape(NX, NZL, NC, NZH, NY), AXES)
    engine, expert = ("x", "zl", "core"), ("zh", "y")
    rows = P(None, AXES, None)
    return jax.shard_map(
        per_device,
        mesh=grid,
        in_specs=(
            rows,
            rows,
            rows,
            P(expert, engine, None),
            P(expert, engine, None),
            P(expert, engine, None),
            P(expert, None, engine),
            P(expert, None, engine),
            P(expert, None, engine),
        ),
        out_specs=rows,
        check_vma=False,
    )
```
